32 devices in a mesh: dp: 2 (over y), row: 4 (over x, core), col: 4 (over z).
Axes of the slice: x: 2, y: 2, z: 4, core: 2. Of those that a mesh axis runs over, the one named last changes fastest.
Arguments:
- grad_out: bfloat16 [512, 8192], P(('dp', 'col'), 'row'), may hold values from -6 to 6
- saved_hidden: bfloat16 [512, 26624], P(('dp', 'row'), 'col'), may hold values from -0.26367188 to 0.26367188
- down_weight: bfloat16 [26624, 8192], P('col', 'row'), may hold values from -0.0625 to 0.0625
Outputs:
- input_grad: bfloat16 [512, 26624], P(('dp', 'row'), 'col')
- weight_grad: bfloat16 [26624, 8192], P(('col', 'dp'), 'row')
The draws below stay inside these ranges and needn't reach their ends.
All inputs are finite; a program needn't handle non-finite values.
Results may differ from the reference program's by a relative error of at most 0.001.
Values may be sent and summed in bfloat16 or wider, within the bound.
No kernel may reach another device: no remote copies, remote signals or barrier semaphores. Data moves between devices by JAX's collectives and lax.ppermute only.
A program may use at most 128 MiB of HBM per device.

```python
import jax
import jax.numpy as jnp

D = 8192
FFW = 26624
TOKENS = 512


def block_levels(stream_key, extent, pieces, least, largest):
    factor_of = 1.0
    for axis_at, shards_of in pieces:
        heights = jax.random.uniform(jax.random.fold_in(jax.random.fold_in(stream_key, 6), axis_at), (shards_of,), jnp.float32, least / len(pieces), largest / len(pieces))
        factor_of = factor_of * jnp.repeat(jnp.exp(heights), extent[axis_at] // shards_of).reshape((-1,) + (1,) * (len(extent) - 1 - axis_at))
    return factor_of


def noise(own_key, dims, spread, most, pieces=(), held_as=jnp.bfloat16):
    entries = jax.random.normal(own_key, dims, jnp.float32) * spread
    if len(pieces) > 0:
        entries = block_levels(own_key, dims, pieces, -0.22, 0.18) * entries
    return jnp.clip(entries, min=-most, max=most).astype(held_as)


def setup_inputs(seed: int = 0) -> dict:
    keys = jax.random.split(jax.random.key(seed), 4)
    return {
        "grad_out": noise(keys[0], (TOKENS, D), 1.0, 6.0, ((0, 8), (1, 4))),
        "saved_hidden": noise(keys[1], (TOKENS, FFW), (TOKENS ** -0.5), 0.26367188, ((0, 8), (1, 4))),
        "down_weight": noise(keys[2], (FFW, D), D ** -0.5, 0.0625, ((0, 4), (1, 4))),
    }


def reference(grad_out, saved_hidden, down_weight):
    input_grad = jnp.dot(grad_out, down_weight.T, preferred_element_type=jnp.float32).astype(jnp.bfloat16)
    weight_grad = jnp.dot(saved_hidden.T, grad_out, preferred_element_type=jnp.float32).astype(jnp.bfloat16)
    return input_grad, weight_grad
```

```python
import jax
import jax.numpy as jnp
from jax import lax
from jax.sharding import PartitionSpec as P

CORES = 2
CHUNKS = 4
GRAD_MOST = 6.0
WEIGHT_MOST = 0.0625
POWER = 8
TOP = 120.0


def native(grad_out, saved_hidden, down_weight):
    local_rows = saved_hidden.shape[0]
    gathered_all = lax.all_gather(grad_out, ("dp", "col"), axis=0, tiled=True)
    copy_count = lax.axis_size("dp")
    row_count = lax.axis_size("row")
    copy_rows = gathered_all.shape[0] // copy_count
    grad_copy = lax.dynamic_slice_in_dim(
        gathered_all, lax.axis_index("dp") * copy_rows, copy_rows, 0
    )
    hidden_parts = lax.all_to_all(saved_hidden, "dp", split_axis=1, concat_axis=0, tiled=True)
    hidden_stack = lax.all_gather(hidden_parts, "row", axis=0, tiled=True)
    hidden_grid = hidden_stack.reshape(row_count, copy_count, local_rows, hidden_stack.shape[1])
    grad_grid = gathered_all.reshape(copy_count, row_count, local_rows, gathered_all.shape[1])
    weight_grad = jnp.einsum(
        "rdtk,drtn->kn", hidden_grid, grad_grid, preferred_element_type=jnp.float32
    )
    input_grad = lax.psum_scatter(
        lax.dot_general(
            grad_copy, down_weight, (((1,), (1,)), ((), ())), preferred_element_type=jnp.float32
        ),
        "row",
        scatter_dimension=0,
        tiled=True,
    )
    return (input_grad.astype(jnp.bfloat16), weight_grad.astype(jnp.bfloat16))


def encode(value, scale):
    scaled = value * scale
    square = scaled * scaled
    fourth = square * square
    eighth = fourth * fourth
    return jnp.where(scaled < 0, -eighth, eighth).astype(jnp.bfloat16)


def decode(code, scale):
    wide = code.astype(jnp.float32)
    root = jnp.sqrt(jnp.sqrt(jnp.sqrt(jnp.abs(wide)))) * (1.0 / scale)
    return jnp.where(wide < 0, -root, root)


def swap(x, axis, mask):
    n = lax.axis_size(axis)
    return lax.ppermute(x, axis, [(i, i ^ mask) for i in range(n)])


def shift(x, axis, by):
    n = lax.axis_size(axis)
    return lax.ppermute(x, axis, [(i, (i + by) % n) for i in range(n)])


def paired(grad_out, saved_hidden, down_weight):
    d, r, z = (lax.axis_index(a) for a in ("dp", "row", "col"))
    n_col = lax.axis_size("col")
    chip = CORES
    rows = saved_hidden.shape[0]
    hid = down_weight.shape[0]
    half = hid // lax.axis_size("dp")
    depth = down_weight.shape[1]

    own = [grad_out] + [shift(grad_out, "col", s) for s in range(1, n_col)]
    h_mine = lax.dynamic_slice_in_dim(saved_hidden, d * half, half, 1)
    h_give = lax.dynamic_slice_in_dim(saved_hidden, (1 - d) * half, half, 1)
    h_peer = swap(h_give, "dp", 1)
    h_far = swap(h_mine, "row", chip)
    h_peer_far = swap(h_peer, "row", chip)
    mine = [h_mine, h_peer, h_far, h_peer_far]
    mate = [swap(h, "row", 1) for h in mine]
    peer = [swap(b, "dp", 1) for b in own]

    def order(blocks):
        stack = jnp.stack(blocks)
        return jnp.concatenate(
            [lax.dynamic_index_in_dim(stack, (z - (r ^ k)) % n_col, 0, False) for k in range(n_col)]
        )

    g_own = order(own)
    scale = 2.0 ** (TOP / POWER) / (CORES * depth * GRAD_MOST * WEIGHT_MOST)
    tiles = hid // 128
    edges = [128 * (tiles * i // CHUNKS) for i in range(CHUNKS + 1)]
    outs = []
    for lo, hi in zip(edges, edges[1:]):
        part = lax.dot_general(
            g_own, down_weight[lo:hi], (((1,), (1,)), ((), ())), preferred_element_type=jnp.float32
        ).reshape(2, CORES, rows, hi - lo)
        give = part[:, 1]
        keep = part[:, 0]
        got = swap(give, "row", 1)
        sent = encode(keep[1] + got[1], scale)
        far = swap(sent, "row", chip)
        outs.append(((keep[0] + got[0]) + decode(far, scale)).astype(jnp.bfloat16))
    input_grad = jnp.concatenate(outs, axis=1)

    hidden = jnp.concatenate([mine[0], mate[0], mine[2], mate[2], mine[1], mate[1], mine[3], mate[3]])
    grads = jnp.concatenate([g_own, order(peer)])
    weight_grad = lax.dot_general(
        hidden, grads, (((0,), (0,)), ((), ())), preferred_element_type=jnp.float32
    ).astype(jnp.bfloat16)
    return input_grad, weight_grad


def local(grad_out, saved_hidden, down_weight):
    sizes = [lax.axis_size(a) for a in ("dp", "row", "col")]
    if sizes[0] == 2 and sizes[1] == 2 * CORES and sizes[2] == sizes[1]:
        return paired(grad_out, saved_hidden, down_weight)
    return native(grad_out, saved_hidden, down_weight)


def solution(mesh):
    placed = (P(("dp", "col"), "row"), P(("dp", "row"), "col"), P("col", "row"))
    return jax.shard_map(
        local,
        mesh=mesh,
        in_specs=placed,
        out_specs=(P(("dp", "row"), "col"), P(("col", "dp"), "row")),
        check_vma=False,
    )
```

```python
import functools

import jax
import jax.numpy as jnp
from jax import lax
from jax.experimental import pallas as pl
from jax.experimental.pallas import tpu as pltpu
from jax.sharding import PartitionSpec as P


CORES = 2
CHUNKS = 4
NT = (((1,), (1,)), ((), ()))
TN = (((0,), (0,)), ((), ()))
SMALL = 12 * 2**20
SPLIT = 4
WIDE_LIMIT = 36 * 2**20
GRAD_MOST = 6.0
WEIGHT_MOST = 0.0625
POWER = 8
TOP = 120.0


def native(grad_out, saved_hidden, down_weight):
    local_rows = saved_hidden.shape[0]
    gathered_all = lax.all_gather(grad_out, ("dp", "col"), axis=0, tiled=True)
    copy_count = lax.axis_size("dp")
    row_count = lax.axis_size("row")
    copy_rows = gathered_all.shape[0] // copy_count
    grad_copy = lax.dynamic_slice_in_dim(
        gathered_all, lax.axis_index("dp") * copy_rows, copy_rows, 0
    )
    hidden_parts = lax.all_to_all(saved_hidden, "dp", split_axis=1, concat_axis=0, tiled=True)
    hidden_stack = lax.all_gather(hidden_parts, "row", axis=0, tiled=True)
    hidden_grid = hidden_stack.reshape(row_count, copy_count, local_rows, hidden_stack.shape[1])
    grad_grid = gathered_all.reshape(copy_count, row_count, local_rows, gathered_all.shape[1])
    weight_grad = jnp.einsum(
        "rdtk,drtn->kn", hidden_grid, grad_grid, preferred_element_type=jnp.float32
    )
    input_grad = lax.psum_scatter(
        lax.dot_general(
            grad_copy, down_weight, (((1,), (1,)), ((), ())), preferred_element_type=jnp.float32
        ),
        "row",
        scatter_dimension=0,
        tiled=True,
    )
    return (input_grad.astype(jnp.bfloat16), weight_grad.astype(jnp.bfloat16))


def encode(value, scale):
    scaled = value * scale
    square = scaled * scaled
    fourth = square * square
    eighth = fourth * fourth
    return jnp.where(scaled < 0, -eighth, eighth).astype(jnp.bfloat16)


def decode(code, scale):
    wide = code.astype(jnp.float32)
    half = lax.rsqrt(jnp.maximum(jnp.abs(wide), 2.0**-126))
    fourth = lax.rsqrt(half)
    root = fourth * lax.rsqrt(fourth) * (1.0 / scale)
    return jnp.where(wide < 0, -root, jnp.where(wide > 0, root, 0.0))


def swap(x, axis, mask):
    n = lax.axis_size(axis)
    return lax.ppermute(x, axis, [(i, i ^ mask) for i in range(n)])


def put_blocks(at, blocks, held):
    rows = blocks[0].shape[0]
    for i, block in enumerate(blocks):
        held[pl.ds(pl.multiple_of(at[i] * rows, rows), rows), :] = block[...]


def load_kernel(corners, w, *refs):
    outs, sem = refs[:-1], refs[-1]
    copies = []
    for (lo, side), out in zip(corners, outs):
        tall, half = out.shape
        step = tall // SPLIT
        for i in range(SPLIT):
            part = w.at[pl.ds(lo + i * step, step), pl.ds(side * half, half)]
            copies.append(pltpu.make_async_copy(part, out.at[pl.ds(i * step, step)], sem.at[len(copies)]))
    for c in copies:
        c.start()
    return copies


def load_only(corners, w, *refs):
    for c in load_kernel(corners, w, *refs):
        c.wait()


def load(weight, corners, tall):
    half = weight.shape[1] // 2
    outs = pl.pallas_call(
        functools.partial(load_only, corners),
        in_specs=[pl.BlockSpec(memory_space=pltpu.HBM)],
        out_specs=[pl.BlockSpec(memory_space=pltpu.VMEM)] * len(corners),
        out_shape=[pltpu.VMEM((tall, half), weight.dtype)] * len(corners),
        scratch_shapes=[pltpu.SemaphoreType.DMA((SPLIT * len(corners),))],
        cost_estimate=pl.CostEstimate(
            flops=0, bytes_accessed=2 * len(corners) * tall * half, transcendentals=0
        ),
        compiler_params=pltpu.CompilerParams(vmem_limit_bytes=SMALL),
    )(pltpu.with_memory_space_constraint(weight, pltpu.HBM))
    return outs


def first_kernel(n, corners, at, b0, b1, b2, b3, w, *refs):
    now, acc, later, held, sem = refs[:n], refs[n], refs[n + 1 : -2], refs[-2], refs[-1]
    copies = load_kernel(corners, w, *later, sem)
    put_blocks(at, (b0, b1, b2, b3), held)
    tall = now[0].shape[0]
    for i, ref in enumerate(now):
        acc[:, i * tall : (i + 1) * tall] = lax.dot_general(
            held[...], ref[...], NT, preferred_element_type=jnp.float32
        )
    for c in copies:
        c.wait()


def first_half(at, blocks, weight, now, corners):
    rows = 4 * blocks[0].shape[0]
    tall, half = now[0].shape
    whole = pl.BlockSpec(memory_space=pltpu.VMEM)
    outs = pl.pallas_call(
        functools.partial(first_kernel, len(now), corners),
        grid=(1,),
        in_specs=[pl.BlockSpec(memory_space=pltpu.SMEM)]
        + [pl.BlockSpec((b.shape[0], half), lambda i: (0, 0)) for b in blocks]
        + [pl.BlockSpec(memory_space=pltpu.HBM)]
        + [whole] * len(now),
        out_specs=[whole] * (1 + len(corners)),
        out_shape=[pltpu.VMEM((rows, tall * len(now)), jnp.float32)]
        + [pltpu.VMEM((tall, half), weight.dtype)] * len(corners),
        scratch_shapes=[
            pltpu.VMEM((rows, half), weight.dtype),
            pltpu.SemaphoreType.DMA((SPLIT * len(corners),)),
        ],
        cost_estimate=pl.CostEstimate(
            flops=2 * rows * tall * len(now) * half,
            bytes_accessed=2 * len(corners) * tall * half,
            transcendentals=0,
        ),
        compiler_params=pltpu.CompilerParams(vmem_limit_bytes=SMALL),
    )(at, *blocks, pltpu.with_memory_space_constraint(weight, pltpu.HBM), *now)
    return outs[0], outs[1:]


def second_kernel(lo, n_now, corners, at, b0, b1, b2, b3, w, *refs):
    n = len(corners)
    now, rest = refs[:n_now], refs[n_now:]
    acc, rest = (rest[0], rest[1:]) if lo is not None else (None, rest)
    keep, give, later, held = rest[0], rest[1], rest[2 : 2 + n], rest[2 + n]
    copies = load_kernel(corners, w, *later, rest[-1]) if n else []
    put_blocks(at, (b0, b1, b2, b3), held)
    top, tall = keep.shape
    half = now[0].shape[1]
    part = lax.dot_general(
        held[:, -half:], now[-1][...], NT, preferred_element_type=jnp.float32
    )
    if acc is None:
        part += lax.dot_general(held[:, :half], now[0][...], NT, preferred_element_type=jnp.float32)
    else:
        part += acc[:, lo : lo + tall]
    keep[...] = part[:top]
    give[...] = part[top:]
    for c in copies:
        c.wait()


def second_half(at, blocks, weight, now, acc, lo, corners=()):
    rows = 4 * blocks[0].shape[0]
    tall, half = now[0].shape
    wide = half * len(now)
    whole = pl.BlockSpec(memory_space=pltpu.VMEM)
    scratch = [pltpu.VMEM((rows, wide), weight.dtype)]
    if corners:
        scratch.append(pltpu.SemaphoreType.DMA((SPLIT * len(corners),)))
    outs = pl.pallas_call(
        functools.partial(second_kernel, None if acc is None else lo, len(now), corners),
        grid=(1,),
        in_specs=[pl.BlockSpec(memory_space=pltpu.SMEM)]
        + [
            pl.BlockSpec((b.shape[0], wide), lambda i, at=b.shape[1] // wide - 1: (0, at))
            for b in blocks
        ]
        + [pl.BlockSpec(memory_space=pltpu.HBM)]
        + [whole] * (len(now) + (acc is not None)),
        out_specs=[whole] * (2 + len(corners)),
        out_shape=[jax.ShapeDtypeStruct((rows // 2, tall), jnp.float32)] * 2
        + [pltpu.VMEM((tall, half), weight.dtype)] * len(corners),
        scratch_shapes=scratch,
        cost_estimate=pl.CostEstimate(
            flops=2 * rows * tall * wide, bytes_accessed=2 * tall * wide, transcendentals=0
        ),
        compiler_params=pltpu.CompilerParams(vmem_limit_bytes=SMALL),
    )(
        at,
        *blocks,
        pltpu.with_memory_space_constraint(weight, pltpu.HBM),
        *now,
        *([] if acc is None else [acc]),
    )
    return outs[0], outs[1], outs[2:]


def finish_kernel(scale, *refs):
    out = refs[-1]
    rows = out.shape[0]
    lo = 0
    for keep, got, far in zip(refs[0:-1:3], refs[1:-1:3], refs[2:-1:3]):
        tall = far.shape[1]
        value = (keep[:rows] + got[:rows]) + decode(far[...], scale)
        out[:, lo : lo + tall] = value.astype(out.dtype)
        lo += tall


def finish(parts, scale, dtype):
    rows = parts[0][2].shape[0]
    whole = pl.BlockSpec(memory_space=pltpu.VMEM)
    hid = sum(p[2].shape[1] for p in parts)
    return pl.pallas_call(
        functools.partial(finish_kernel, scale),
        in_specs=[whole] * (3 * len(parts)),
        out_specs=whole,
        out_shape=jax.ShapeDtypeStruct((rows, hid), dtype),
        cost_estimate=pl.CostEstimate(
            flops=20 * rows * hid, bytes_accessed=14 * rows * hid, transcendentals=0
        ),
        compiler_params=pltpu.CompilerParams(vmem_limit_bytes=SMALL),
    )(*[x for p in parts for x in p])


def weight_kernel(counts, at, *refs):
    rows = refs[0].shape[0]
    n_hid, n_grad = len(counts), sum(counts)
    hidden, grads, out, held = refs[:n_hid], refs[n_hid : n_hid + n_grad], *refs[-2:]
    wide = out.shape[1]

    @pl.when((pl.program_id(0) == 0) & (pl.program_id(1) == 0))
    def _():
        left = list(grads)
        for i, count in enumerate(counts):
            place = at[i % 4] + 4 * (i // 4)
            lanes = 0
            for piece in left[:count]:
                span = piece.shape[1]
                start = pl.multiple_of(place * rows, rows)
                held[pl.ds(start, rows), lanes : lanes + span] = piece[...]
                lanes += span
            left = left[count:]

    stacked = jnp.concatenate([h[...] for h in hidden])
    start = pl.multiple_of(pl.program_id(1) * wide, wide)
    out[...] = lax.dot_general(
        stacked, held[:, pl.ds(start, wide)], TN, preferred_element_type=jnp.float32
    ).astype(out.dtype)


def weight_product(at, hidden, grads):
    pieces = [g if isinstance(g, tuple) else (g,) for g in grads]
    rows, hid = hidden[0].shape
    depth = sum(p.shape[1] for p in pieces[0])
    tall, wide = hid // 2, depth // 2
    tokens = rows * len(hidden)
    flat = [p for group in pieces for p in group]
    return pl.pallas_call(
        functools.partial(weight_kernel, [len(p) for p in pieces]),
        grid=(hid // tall, depth // wide),
        in_specs=[pl.BlockSpec(memory_space=pltpu.SMEM)]
        + [pl.BlockSpec((rows, tall), lambda i, j: (0, i)) for _ in hidden]
        + [pl.BlockSpec(p.shape, lambda i, j: (0, 0)) for p in flat],
        out_specs=pl.BlockSpec((tall, wide), lambda i, j: (i, j)),
        out_shape=jax.ShapeDtypeStruct((hid, depth), hidden[0].dtype),
        scratch_shapes=[pltpu.VMEM((tokens, depth), hidden[0].dtype)],
        cost_estimate=pl.CostEstimate(
            flops=2 * tokens * hid * depth, bytes_accessed=2 * hid * depth, transcendentals=0
        ),
        compiler_params=pltpu.CompilerParams(vmem_limit_bytes=WIDE_LIMIT),
    )(at, *hidden, *flat)


def paired(grad_out, saved_hidden, down_weight):
    d, r, z = (lax.axis_index(a) for a in ("dp", "row", "col"))
    chip = CORES
    rows = saved_hidden.shape[0]
    hid, depth = down_weight.shape
    half = hid // 2
    cut = depth // 2

    h_give = lax.dynamic_slice_in_dim(saved_hidden, (1 - d) * half, half, 1)
    h_peer = swap(h_give, "dp", 1)
    rev_a = swap(grad_out[:, :cut], "col", 3)
    pair = swap(grad_out, "col", 1)
    h_mine = lax.dynamic_slice_in_dim(saved_hidden, d * half, half, 1)
    h_far = swap(h_mine, "row", chip)
    rev_b = swap(grad_out[:, cut:], "col", 3)
    y_own = swap(grad_out, "dp", 1)
    s2_a = swap(rev_a, "col", 1)
    s2_b = swap(rev_b, "col", 1)
    h_peer_far = swap(h_peer, "row", chip)
    y_pair = swap(pair, "dp", 1)
    rev = jnp.concatenate([rev_a, rev_b], 1)
    s2 = jnp.concatenate([s2_a, s2_b], 1)
    y_rev = swap(rev, "dp", 1)
    y_s2 = swap(y_rev, "col", 1)
    mine = [h_mine, h_peer, h_far, h_peer_far]
    mate = [swap(h, "row", 1) for h in mine]

    ks = [r ^ z ^ m for m in (0, 1, 3, 2)]
    at = jnp.stack([((k & 1) << 1) | (k >> 1) for k in ks]).astype(jnp.int32)
    scale = 2.0 ** (TOP / POWER) / (CORES * depth * GRAD_MOST * WEIGHT_MOST)
    tall = hid // CHUNKS
    spots = [i * tall for i in range(CHUNKS)]
    early = CHUNKS - 1
    held = {}

    def fetch(keys, outs):
        held.update(zip(keys, outs))

    plan = [(i, s) for s in range(2) for i in range(early)]
    groups = [plan[:2], plan[2:4], plan[4:]]
    at_corner = [[(spots[i], s) for i, s in g] for g in groups]
    for n in range(2):
        fetch(groups[n], load(down_weight, at_corner[n], tall))
    now = [held[i, 0] for i in range(early)]
    acc, outs = first_half(at, (grad_out, pair, rev_a, s2_a), down_weight, now, at_corner[2])
    fetch(groups[2], outs)
    parts = []
    for i, lo in enumerate(spots):
        if i < early:
            keys = [(early, i - 1)] if i else []
            corners = [(spots[early], s) for _, s in keys]
            blocks = (grad_out, pair, rev_b, s2_b)
            keep, give, outs = second_half(at, blocks, down_weight, [held[i, 1]], acc, lo, corners)
            fetch(keys, outs)
        else:
            blocks = (grad_out, pair, rev, s2)
            now = [held[early, s] for s in range(2)]
            keep, give, _ = second_half(at, blocks, down_weight, now, None, lo)
        got = swap(give, "row", 1)
        sent = encode(keep[rows:] + got[rows:], scale)
        parts.append((keep, got, swap(sent, "row", chip)))
    input_grad = finish(parts, scale, saved_hidden.dtype)

    weight_grad = weight_product(
        at,
        [mine[0], mine[2], mate[0], mate[2], mine[1], mine[3], mate[1], mate[3]],
        [grad_out, pair, rev, s2, y_own, y_pair, y_rev, y_s2],
    )
    return input_grad, weight_grad


def local(grad_out, saved_hidden, down_weight):
    sizes = [lax.axis_size(a) for a in ("dp", "row", "col")]
    if sizes[0] == 2 and sizes[1] == 2 * CORES and sizes[2] == sizes[1]:
        return paired(grad_out, saved_hidden, down_weight)
    return native(grad_out, saved_hidden, down_weight)


def solution(mesh):
    placed = (P(("dp", "col"), "row"), P(("dp", "row"), "col"), P("col", "row"))
    return jax.shard_map(
        local,
        mesh=mesh,
        in_specs=placed,
        out_specs=(P(("dp", "row"), "col"), P(("col", "dp"), "row")),
        check_vma=False,
    )
```

```python
import functools

import jax
import jax.numpy as jnp
from jax import lax
from jax.experimental import pallas as pl
from jax.experimental.pallas import tpu as pltpu
from jax.sharding import PartitionSpec as P


CORES = 2
LOADS = 3
EARLY = 1
STEPS = (8, 8, 6, 4)
ACROSS = 1
SHARES = (17, 17, 18)
CHUNKS = len(SHARES)
NT = (((1,), (1,)), ((), ()))
TN = (((0,), (0,)), ((), ()))
SMALL = 12 * 2**20
SPLIT = 8
LANES = 128
WIDE_LIMIT = 28 * 2**20
GRAD_MOST = 6.0
WEIGHT_MOST = 0.0625
POWER = 8
TOP = 120.0


def native(grad_out, saved_hidden, down_weight):
    local_rows = saved_hidden.shape[0]
    gathered_all = lax.all_gather(grad_out, ("dp", "col"), axis=0, tiled=True)
    copy_count = lax.axis_size("dp")
    row_count = lax.axis_size("row")
    copy_rows = gathered_all.shape[0] // copy_count
    grad_copy = lax.dynamic_slice_in_dim(
        gathered_all, lax.axis_index("dp") * copy_rows, copy_rows, 0
    )
    hidden_parts = lax.all_to_all(saved_hidden, "dp", split_axis=1, concat_axis=0, tiled=True)
    hidden_stack = lax.all_gather(hidden_parts, "row", axis=0, tiled=True)
    hidden_grid = hidden_stack.reshape(row_count, copy_count, local_rows, hidden_stack.shape[1])
    grad_grid = gathered_all.reshape(copy_count, row_count, local_rows, gathered_all.shape[1])
    weight_grad = jnp.einsum(
        "rdtk,drtn->kn", hidden_grid, grad_grid, preferred_element_type=jnp.float32
    )
    input_grad = lax.psum_scatter(
        lax.dot_general(
            grad_copy, down_weight, (((1,), (1,)), ((), ())), preferred_element_type=jnp.float32
        ),
        "row",
        scatter_dimension=0,
        tiled=True,
    )
    return (input_grad.astype(jnp.bfloat16), weight_grad.astype(jnp.bfloat16))


def encode(value, scale):
    scaled = value * scale
    square = scaled * scaled
    fourth = square * square
    eighth = fourth * fourth
    return jnp.where(scaled < 0, -eighth, eighth).astype(jnp.bfloat16)


def decode(code, scale):
    wide = code.astype(jnp.float32)
    half = lax.rsqrt(jnp.maximum(jnp.abs(wide), 2.0**-126))
    fourth = lax.rsqrt(half)
    root = fourth * lax.rsqrt(fourth) * (1.0 / scale)
    return jnp.where(wide < 0, -root, jnp.where(wide > 0, root, 0.0))


def swap(x, axis, mask):
    n = lax.axis_size(axis)
    return lax.ppermute(x, axis, [(i, i ^ mask) for i in range(n)])


def put_blocks(at, blocks, held):
    rows = blocks[0].shape[0]
    for i, block in enumerate(blocks):
        held[pl.ds(pl.multiple_of(at[i] * rows, rows), rows), :] = block[...]


def start_loads(spans, w, outs, sem):
    copies = []
    for (lo, hi), out in zip(spans, outs):
        step = (hi - lo) // SPLIT
        for i in range(SPLIT):
            part = w.at[pl.ds(lo + i * step, step)]
            copies.append(pltpu.make_async_copy(part, out.at[pl.ds(i * step, step)], sem.at[len(copies)]))
    for c in copies:
        c.start()
    return copies


def load_kernel(spans, at, w, *refs):
    del at
    for c in start_loads(spans, w, refs[:-1], refs[-1]):
        c.wait()


def load(at, weight, spans):
    depth = weight.shape[1]
    return pl.pallas_call(
        functools.partial(load_kernel, spans),
        in_specs=[pl.BlockSpec(memory_space=pltpu.SMEM), pl.BlockSpec(memory_space=pltpu.HBM)],
        out_specs=[pl.BlockSpec(memory_space=pltpu.VMEM)] * len(spans),
        out_shape=[pltpu.VMEM((hi - lo, depth), weight.dtype) for lo, hi in spans],
        scratch_shapes=[pltpu.SemaphoreType.DMA((SPLIT * len(spans),))],
        cost_estimate=pl.CostEstimate(
            flops=0, bytes_accessed=2 * depth * sum(hi - lo for lo, hi in spans), transcendentals=0
        ),
        compiler_params=pltpu.CompilerParams(vmem_limit_bytes=SMALL),
    )(at, pltpu.with_memory_space_constraint(weight, pltpu.HBM))


def product_kernel(n_block, spans, *refs):
    if n_block:
        at, refs = refs[0], refs[1:]
    n = max(n_block, 1)
    blocks, now, refs = refs[:n], refs[n : n + len(spans)], refs[n + len(spans) :]
    keep, give = refs[:2]
    held = blocks[0]
    if n_block:
        held = refs[2]
        put_blocks(at, blocks, held)
    top = keep.shape[0]
    lo = 0
    for ref, (first, last) in zip(now, spans):
        hi = lo + last - first
        part = lax.dot_general(
            held[...], ref[first:last, :], NT, preferred_element_type=jnp.float32
        )
        keep[:, lo:hi] = part[:top]
        give[:, lo:hi] = part[top:]
        lo = hi


def product(grads, now):
    at, blocks = grads if isinstance(grads, tuple) else (None, [])
    rows = 4 * blocks[0].shape[0] if blocks else grads.shape[0]
    depth = now[0][2].shape[1]
    spans = [(first, last) for first, last, _ in now]
    tall = sum(last - first for first, last in spans)
    whole = pl.BlockSpec(memory_space=pltpu.VMEM)
    outs = pl.pallas_call(
        functools.partial(product_kernel, len(blocks), spans),
        in_specs=[pl.BlockSpec(memory_space=pltpu.SMEM)] * (at is not None)
        + [whole] * (max(len(blocks), 1) + len(now)),
        out_specs=[whole] * (2 + (at is not None)),
        out_shape=[jax.ShapeDtypeStruct((rows // 2, tall), jnp.float32)] * 2
        + [pltpu.VMEM((rows, depth), now[0][2].dtype)] * (at is not None),
        cost_estimate=pl.CostEstimate(
            flops=2 * rows * tall * depth, bytes_accessed=2 * tall * depth, transcendentals=0
        ),
        compiler_params=pltpu.CompilerParams(vmem_limit_bytes=SMALL),
    )(
        *([] if at is None else [at]),
        *(blocks or [grads]),
        *[pltpu.with_memory_space_constraint(w, pltpu.VMEM) for _, _, w in now],
    )
    return outs[0], outs[1], outs[-1] if blocks else grads


def finish_kernel(scale, ready, *refs):
    done, refs, (out, staged, sem) = refs[:ready], refs[ready:-3], refs[-3:]
    rows = out.shape[0]
    copies = []
    lo = 0

    def write(tall):
        window = pl.ds(lo, tall)
        copies.append(
            pltpu.make_async_copy(staged.at[:, window], out.at[:, window], sem.at[len(copies)])
        )
        copies[-1].start()

    for chunk in done:
        tall = chunk.shape[1]
        staged[:, lo : lo + tall] = chunk[...]
        write(tall)
        lo += tall
    for keep, got, far in zip(refs[0::3], refs[1::3], refs[2::3]):
        tall = far.shape[1]
        value = (keep[:rows] + got[:rows]) + decode(far[...], scale)
        staged[:, lo : lo + tall] = value.astype(staged.dtype)
        write(tall)
        lo += tall
    for c in copies:
        c.wait()


def finish(done, parts, scale, dtype):
    rows = parts[0][2].shape[0]
    whole = pl.BlockSpec(memory_space=pltpu.VMEM)
    hid = sum(c.shape[1] for c in done) + sum(p[2].shape[1] for p in parts)
    return pl.pallas_call(
        functools.partial(finish_kernel, scale, len(done)),
        in_specs=[whole] * (len(done) + 3 * len(parts)),
        out_specs=pl.BlockSpec(memory_space=pltpu.HBM),
        out_shape=jax.ShapeDtypeStruct((rows, hid), dtype),
        scratch_shapes=[
            pltpu.VMEM((rows, hid), dtype),
            pltpu.SemaphoreType.DMA((len(done) + len(parts),)),
        ],
        cost_estimate=pl.CostEstimate(
            flops=20 * rows * hid, bytes_accessed=14 * rows * hid, transcendentals=0
        ),
        compiler_params=pltpu.CompilerParams(vmem_limit_bytes=SMALL),
    )(*done, *[x for p in parts for x in p])


def early_kernel(scale, keep, got, far, out):
    rows = out.shape[0]
    out[...] = ((keep[:rows] + got[:rows]) + decode(far[...], scale)).astype(out.dtype)


def early(part, scale, dtype):
    rows, tall = part[2].shape
    whole = pl.BlockSpec(memory_space=pltpu.VMEM)
    return pl.pallas_call(
        functools.partial(early_kernel, scale),
        in_specs=[whole] * 3,
        out_specs=whole,
        out_shape=pltpu.VMEM((rows, tall), dtype),
        cost_estimate=pl.CostEstimate(
            flops=20 * rows * tall, bytes_accessed=14 * rows * tall, transcendentals=0
        ),
        compiler_params=pltpu.CompilerParams(vmem_limit_bytes=SMALL),
    )(*part)


def weight_kernel(n_hid, pieces, at, *refs):
    rows = refs[0].shape[0]
    hidden, own, peers = refs[:n_hid], refs[n_hid], refs[n_hid + 1 : -4]
    out, held, slots, sem = refs[-4:]
    half = own.shape[0]
    held[:half, :] = own[...]
    for peer, places in zip(peers, ((0, 2), (1,), (3,))):
        for i, place in enumerate(places):
            start = pl.multiple_of(half + at[place] * rows, rows)
            held[pl.ds(start, rows), :] = peer[i * rows : (i + 1) * rows]
    copies = []
    for n, (top, end, lo, hi) in enumerate(pieces):
        if n >= 2:
            copies[n - 2].wait()
        stacked = jnp.concatenate([h[:, top:end] for h in hidden])
        slot = slots.at[n % 2, : end - top, : hi - lo]
        slot[...] = lax.dot_general(
            stacked, held[:, lo:hi], TN, preferred_element_type=jnp.float32
        ).astype(out.dtype)
        place = out.at[pl.ds(top, end - top), pl.ds(lo, hi - lo)]
        copies.append(pltpu.make_async_copy(slot, place, sem.at[n]))
        copies[-1].start()
    for c in copies[-2:]:
        c.wait()


def weight_product(at, hidden, own, peers):
    rows, hid = hidden[0].shape
    depth = own.shape[1]
    tokens = rows * len(hidden)
    tiles = hid // LANES
    edges = [LANES * (tiles * sum(STEPS[:i]) // sum(STEPS)) for i in range(len(STEPS) + 1)]
    pieces = [(top, end, lo, lo + depth // ACROSS) for top, end in zip(edges, edges[1:]) for lo in range(0, depth, depth // ACROSS)]
    tall, wide = max(end - top for top, end, _, _ in pieces), depth // ACROSS
    whole = pl.BlockSpec(memory_space=pltpu.VMEM)
    return pl.pallas_call(
        functools.partial(weight_kernel, len(hidden), pieces),
        in_specs=[pl.BlockSpec(memory_space=pltpu.SMEM)] + [whole] * (len(hidden) + 1 + len(peers)),
        out_specs=pl.BlockSpec(memory_space=pltpu.HBM),
        out_shape=jax.ShapeDtypeStruct((hid, depth), hidden[0].dtype),
        scratch_shapes=[
            pltpu.VMEM((tokens, depth), hidden[0].dtype),
            pltpu.VMEM((2, tall, wide), hidden[0].dtype),
            pltpu.SemaphoreType.DMA((len(pieces),)),
        ],
        cost_estimate=pl.CostEstimate(
            flops=2 * tokens * hid * depth, bytes_accessed=2 * hid * depth, transcendentals=0
        ),
        compiler_params=pltpu.CompilerParams(vmem_limit_bytes=WIDE_LIMIT),
    )(at, *hidden, own, *peers)


def paired(grad_out, saved_hidden, down_weight):
    d, r, z = (lax.axis_index(a) for a in ("dp", "row", "col"))
    chip = CORES
    rows = saved_hidden.shape[0]
    hid, depth = down_weight.shape
    half = hid // 2

    pair = swap(grad_out, "col", 1)
    rev = swap(grad_out, "col", 3)
    s2 = swap(rev, "col", 1)
    two = jnp.concatenate([grad_out, rev])
    y_two = swap(two, "dp", 1)
    y_pair = swap(pair, "dp", 1)
    y_rev = y_two[grad_out.shape[0] :]
    y_s2 = swap(y_rev, "col", 1)
    h_give = lax.dynamic_slice_in_dim(saved_hidden, (1 - d) * half, half, 1)
    h_mine = lax.dynamic_slice_in_dim(saved_hidden, d * half, half, 1)
    h_peer = swap(h_give, "dp", 1)
    h_far = swap(h_mine, "row", chip)
    h_peer_far = swap(h_peer, "row", chip)
    mine = [h_mine, h_peer, h_far, h_peer_far]
    mate = [swap(h, "row", 1) for h in mine]

    ks = [r ^ z ^ m for m in (0, 1, 3, 2)]
    at = jnp.stack([((k & 1) << 1) | (k >> 1) for k in ks]).astype(jnp.int32)
    scale = 2.0 ** (TOP / POWER) / (CORES * depth * GRAD_MOST * WEIGHT_MOST)
    tiles = hid // LANES
    edges = [LANES * (tiles * sum(SHARES[:i]) // sum(SHARES)) for i in range(CHUNKS + 1)]
    cuts = [LANES * (tiles * i // LOADS) for i in range(LOADS + 1)]
    loaded = []
    for lo, hi in zip(cuts, cuts[1:]):
        (part,) = load(at, down_weight, [(lo, hi)])
        loaded.append((lo, hi, part))
    grads = (at, [grad_out, pair, rev, s2])
    parts = []
    for lo, hi in zip(edges, edges[1:]):
        now = [(max(lo, a) - a, min(hi, b) - a, w) for a, b, w in loaded if a < hi and lo < b]
        keep, give, grads = product(grads, now)
        got = swap(give, "row", 1)
        sent = encode(keep[rows:] + got[rows:], scale)
        parts.append((keep, got, swap(sent, "row", chip)))
    done = [early(part, scale, saved_hidden.dtype) for part in parts[:EARLY]]
    input_grad = finish(done, parts[EARLY:], scale, saved_hidden.dtype)
    weight_grad = weight_product(
        at,
        [mine[0], mine[2], mate[0], mate[2], mine[1], mine[3], mate[1], mate[3]],
        grads,
        [y_two, y_pair, y_s2],
    )
    return input_grad, weight_grad


def local(grad_out, saved_hidden, down_weight):
    sizes = [lax.axis_size(a) for a in ("dp", "row", "col")]
    if sizes[0] == 2 and sizes[1] == 2 * CORES and sizes[2] == sizes[1]:
        return paired(grad_out, saved_hidden, down_weight)
    return native(grad_out, saved_hidden, down_weight)


def solution(mesh):
    placed = (P(("dp", "col"), "row"), P(("dp", "row"), "col"), P("col", "row"))
    return jax.shard_map(
        local,
        mesh=mesh,
        in_specs=placed,
        out_specs=(P(("dp", "row"), "col"), P(("col", "dp"), "row")),
        check_vma=False,
    )
```

```python
import functools

import jax
import jax.numpy as jnp
from jax import lax
from jax.experimental import pallas as pl
from jax.experimental.pallas import tpu as pltpu
from jax.sharding import PartitionSpec as P


CORES = 2
LOADS = 3
EARLY = 1
STEPS = (8, 8, 6, 4)
ACROSS = 1
SHARES = (12, 13, 13, 14)
CHUNKS = len(SHARES)
NT = (((1,), (1,)), ((), ()))
TN = (((0,), (0,)), ((), ()))
SMALL = 12 * 2**20
SPLIT = 8
LANES = 128
WIDE_LIMIT = 28 * 2**20
GRAD_MOST = 6.0
WEIGHT_MOST = 0.0625
POWER = 8
TOP = 120.0


def native(grad_out, saved_hidden, down_weight):
    local_rows = saved_hidden.shape[0]
    gathered_all = lax.all_gather(grad_out, ("dp", "col"), axis=0, tiled=True)
    copy_count = lax.axis_size("dp")
    row_count = lax.axis_size("row")
    copy_rows = gathered_all.shape[0] // copy_count
    grad_copy = lax.dynamic_slice_in_dim(
        gathered_all, lax.axis_index("dp") * copy_rows, copy_rows, 0
    )
    hidden_parts = lax.all_to_all(saved_hidden, "dp", split_axis=1, concat_axis=0, tiled=True)
    hidden_stack = lax.all_gather(hidden_parts, "row", axis=0, tiled=True)
    hidden_grid = hidden_stack.reshape(row_count, copy_count, local_rows, hidden_stack.shape[1])
    grad_grid = gathered_all.reshape(copy_count, row_count, local_rows, gathered_all.shape[1])
    weight_grad = jnp.einsum(
        "rdtk,drtn->kn", hidden_grid, grad_grid, preferred_element_type=jnp.float32
    )
    input_grad = lax.psum_scatter(
        lax.dot_general(
            grad_copy, down_weight, (((1,), (1,)), ((), ())), preferred_element_type=jnp.float32
        ),
        "row",
        scatter_dimension=0,
        tiled=True,
    )
    return (input_grad.astype(jnp.bfloat16), weight_grad.astype(jnp.bfloat16))


def encode(value, scale):
    scaled = value * scale
    square = scaled * scaled
    fourth = square * square
    eighth = fourth * fourth
    return jnp.where(scaled < 0, -eighth, eighth).astype(jnp.bfloat16)


def decode(code, scale):
    wide = code.astype(jnp.float32)
    half = lax.rsqrt(jnp.maximum(jnp.abs(wide), 2.0**-126))
    fourth = lax.rsqrt(half)
    root = fourth * lax.rsqrt(fourth) * (1.0 / scale)
    return jnp.where(wide < 0, -root, jnp.where(wide > 0, root, 0.0))


def swap(x, axis, mask):
    n = lax.axis_size(axis)
    return lax.ppermute(x, axis, [(i, i ^ mask) for i in range(n)])


def put_blocks(at, blocks, held):
    rows = blocks[0].shape[0]
    for i, block in enumerate(blocks):
        held[pl.ds(pl.multiple_of(at[i] * rows, rows), rows), :] = block[...]


def start_loads(spans, w, outs, sem):
    copies = []
    for (lo, hi), out in zip(spans, outs):
        step = (hi - lo) // SPLIT
        for i in range(SPLIT):
            part = w.at[pl.ds(lo + i * step, step)]
            copies.append(pltpu.make_async_copy(part, out.at[pl.ds(i * step, step)], sem.at[len(copies)]))
    for c in copies:
        c.start()
    return copies


def load_kernel(spans, at, w, *refs):
    del at
    for c in start_loads(spans, w, refs[:-1], refs[-1]):
        c.wait()


def load(at, weight, spans):
    depth = weight.shape[1]
    return pl.pallas_call(
        functools.partial(load_kernel, spans),
        in_specs=[pl.BlockSpec(memory_space=pltpu.SMEM), pl.BlockSpec(memory_space=pltpu.HBM)],
        out_specs=[pl.BlockSpec(memory_space=pltpu.VMEM)] * len(spans),
        out_shape=[pltpu.VMEM((hi - lo, depth), weight.dtype) for lo, hi in spans],
        scratch_shapes=[pltpu.SemaphoreType.DMA((SPLIT * len(spans),))],
        cost_estimate=pl.CostEstimate(
            flops=0, bytes_accessed=2 * depth * sum(hi - lo for lo, hi in spans), transcendentals=0
        ),
        compiler_params=pltpu.CompilerParams(vmem_limit_bytes=SMALL),
    )(at, pltpu.with_memory_space_constraint(weight, pltpu.HBM))


def product_kernel(n_block, spans, *refs):
    if n_block:
        at, refs = refs[0], refs[1:]
    n = max(n_block, 1)
    blocks, now, refs = refs[:n], refs[n : n + len(spans)], refs[n + len(spans) :]
    keep, give = refs[:2]
    held = blocks[0]
    if n_block:
        held = refs[2]
        put_blocks(at, blocks, held)
    top = keep.shape[0]
    lo = 0
    for ref, (first, last) in zip(now, spans):
        hi = lo + last - first
        part = lax.dot_general(
            held[...], ref[first:last, :], NT, preferred_element_type=jnp.float32
        )
        keep[:, lo:hi] = part[:top]
        give[:, lo:hi] = part[top:]
        lo = hi


def product(grads, now):
    at, blocks = grads if isinstance(grads, tuple) else (None, [])
    rows = 4 * blocks[0].shape[0] if blocks else grads.shape[0]
    depth = now[0][2].shape[1]
    spans = [(first, last) for first, last, _ in now]
    tall = sum(last - first for first, last in spans)
    whole = pl.BlockSpec(memory_space=pltpu.VMEM)
    outs = pl.pallas_call(
        functools.partial(product_kernel, len(blocks), spans),
        in_specs=[pl.BlockSpec(memory_space=pltpu.SMEM)] * (at is not None)
        + [whole] * (max(len(blocks), 1) + len(now)),
        out_specs=[whole] * (2 + (at is not None)),
        out_shape=[jax.ShapeDtypeStruct((rows // 2, tall), jnp.float32)] * 2
        + [pltpu.VMEM((rows, depth), now[0][2].dtype)] * (at is not None),
        cost_estimate=pl.CostEstimate(
            flops=2 * rows * tall * depth, bytes_accessed=2 * tall * depth, transcendentals=0
        ),
        compiler_params=pltpu.CompilerParams(vmem_limit_bytes=SMALL),
    )(
        *([] if at is None else [at]),
        *(blocks or [grads]),
        *[pltpu.with_memory_space_constraint(w, pltpu.VMEM) for _, _, w in now],
    )
    return outs[0], outs[1], outs[-1] if blocks else grads


def finish_kernel(scale, ready, *refs):
    done, refs, (out, staged, sem) = refs[:ready], refs[ready:-3], refs[-3:]
    rows = out.shape[0]
    copies = []
    lo = 0

    def write(tall):
        window = pl.ds(lo, tall)
        copies.append(
            pltpu.make_async_copy(staged.at[:, window], out.at[:, window], sem.at[len(copies)])
        )
        copies[-1].start()

    for chunk in done:
        tall = chunk.shape[1]
        staged[:, lo : lo + tall] = chunk[...]
        write(tall)
        lo += tall
    for keep, got, far in zip(refs[0::3], refs[1::3], refs[2::3]):
        tall = far.shape[1]
        value = (keep[:rows] + got[:rows]) + decode(far[...], scale)
        staged[:, lo : lo + tall] = value.astype(staged.dtype)
        write(tall)
        lo += tall
    for c in copies:
        c.wait()


def finish(done, parts, scale, dtype):
    rows = parts[0][2].shape[0]
    whole = pl.BlockSpec(memory_space=pltpu.VMEM)
    hid = sum(c.shape[1] for c in done) + sum(p[2].shape[1] for p in parts)
    return pl.pallas_call(
        functools.partial(finish_kernel, scale, len(done)),
        in_specs=[whole] * (len(done) + 3 * len(parts)),
        out_specs=pl.BlockSpec(memory_space=pltpu.HBM),
        out_shape=jax.ShapeDtypeStruct((rows, hid), dtype),
        scratch_shapes=[
            pltpu.VMEM((rows, hid), dtype),
            pltpu.SemaphoreType.DMA((len(done) + len(parts),)),
        ],
        cost_estimate=pl.CostEstimate(
            flops=20 * rows * hid, bytes_accessed=14 * rows * hid, transcendentals=0
        ),
        compiler_params=pltpu.CompilerParams(vmem_limit_bytes=SMALL),
    )(*done, *[x for p in parts for x in p])


def early_kernel(scale, keep, got, far, out):
    rows = out.shape[0]
    out[...] = ((keep[:rows] + got[:rows]) + decode(far[...], scale)).astype(out.dtype)


def early(part, scale, dtype):
    rows, tall = part[2].shape
    whole = pl.BlockSpec(memory_space=pltpu.VMEM)
    return pl.pallas_call(
        functools.partial(early_kernel, scale),
        in_specs=[whole] * 3,
        out_specs=whole,
        out_shape=pltpu.VMEM((rows, tall), dtype),
        cost_estimate=pl.CostEstimate(
            flops=20 * rows * tall, bytes_accessed=14 * rows * tall, transcendentals=0
        ),
        compiler_params=pltpu.CompilerParams(vmem_limit_bytes=SMALL),
    )(*part)


def weight_kernel(n_hid, pieces, at, *refs):
    rows = refs[0].shape[0]
    hidden, own, peers = refs[:n_hid], refs[n_hid], refs[n_hid + 1 : -4]
    out, held, slots, sem = refs[-4:]
    half = own.shape[0]
    held[:half, :] = own[...]
    for peer, places in zip(peers, ((0, 2, 1), (3,))):
        for i, place in enumerate(places):
            start = pl.multiple_of(half + at[place] * rows, rows)
            held[pl.ds(start, rows), :] = peer[i * rows : (i + 1) * rows]
    copies = []
    for n, (top, end, lo, hi) in enumerate(pieces):
        if n >= 2:
            copies[n - 2].wait()
        stacked = jnp.concatenate([h[:, top:end] for h in hidden])
        slot = slots.at[n % 2, : end - top, : hi - lo]
        slot[...] = lax.dot_general(
            stacked, held[:, lo:hi], TN, preferred_element_type=jnp.float32
        ).astype(out.dtype)
        place = out.at[pl.ds(top, end - top), pl.ds(lo, hi - lo)]
        copies.append(pltpu.make_async_copy(slot, place, sem.at[n]))
        copies[-1].start()
    for c in copies[-2:]:
        c.wait()


def weight_product(at, hidden, own, peers):
    rows, hid = hidden[0].shape
    depth = own.shape[1]
    tokens = rows * len(hidden)
    tiles = hid // LANES
    edges = [LANES * (tiles * sum(STEPS[:i]) // sum(STEPS)) for i in range(len(STEPS) + 1)]
    pieces = [(top, end, lo, lo + depth // ACROSS) for top, end in zip(edges, edges[1:]) for lo in range(0, depth, depth // ACROSS)]
    tall, wide = max(end - top for top, end, _, _ in pieces), depth // ACROSS
    whole = pl.BlockSpec(memory_space=pltpu.VMEM)
    return pl.pallas_call(
        functools.partial(weight_kernel, len(hidden), pieces),
        in_specs=[pl.BlockSpec(memory_space=pltpu.SMEM)] + [whole] * (len(hidden) + 1 + len(peers)),
        out_specs=pl.BlockSpec(memory_space=pltpu.HBM),
        out_shape=jax.ShapeDtypeStruct((hid, depth), hidden[0].dtype),
        scratch_shapes=[
            pltpu.VMEM((tokens, depth), hidden[0].dtype),
            pltpu.VMEM((2, tall, wide), hidden[0].dtype),
            pltpu.SemaphoreType.DMA((len(pieces),)),
        ],
        cost_estimate=pl.CostEstimate(
            flops=2 * tokens * hid * depth, bytes_accessed=2 * hid * depth, transcendentals=0
        ),
        compiler_params=pltpu.CompilerParams(vmem_limit_bytes=WIDE_LIMIT),
    )(at, *hidden, own, *peers)


def paired(grad_out, saved_hidden, down_weight):
    d, r, z = (lax.axis_index(a) for a in ("dp", "row", "col"))
    chip = CORES
    rows = saved_hidden.shape[0]
    hid, depth = down_weight.shape
    half = hid // 2

    pair = swap(grad_out, "col", 1)
    rev = swap(grad_out, "col", 3)
    s2 = swap(rev, "col", 1)
    three = jnp.concatenate([grad_out, rev, pair])
    y_three = swap(three, "dp", 1)
    y_s2 = swap(s2, "dp", 1)
    h_give = lax.dynamic_slice_in_dim(saved_hidden, (1 - d) * half, half, 1)
    h_mine = lax.dynamic_slice_in_dim(saved_hidden, d * half, half, 1)
    h_peer = swap(h_give, "dp", 1)
    h_far = swap(h_mine, "row", chip)
    h_peer_far = swap(h_peer, "row", chip)
    mine = [h_mine, h_peer, h_far, h_peer_far]
    mate = [swap(h, "row", 1) for h in mine]

    ks = [r ^ z ^ m for m in (0, 1, 3, 2)]
    at = jnp.stack([((k & 1) << 1) | (k >> 1) for k in ks]).astype(jnp.int32)
    scale = 2.0 ** (TOP / POWER) / (CORES * depth * GRAD_MOST * WEIGHT_MOST)
    tiles = hid // LANES
    edges = [LANES * (tiles * sum(SHARES[:i]) // sum(SHARES)) for i in range(CHUNKS + 1)]
    cuts = [LANES * (tiles * i // LOADS) for i in range(LOADS + 1)]
    loaded = []
    for lo, hi in zip(cuts, cuts[1:]):
        (part,) = load(at, down_weight, [(lo, hi)])
        loaded.append((lo, hi, part))
    grads = (at, [grad_out, pair, rev, s2])
    parts = []
    for lo, hi in zip(edges, edges[1:]):
        now = [(max(lo, a) - a, min(hi, b) - a, w) for a, b, w in loaded if a < hi and lo < b]
        keep, give, grads = product(grads, now)
        got = swap(give, "row", 1)
        sent = encode(keep[rows:] + got[rows:], scale)
        parts.append((keep, got, swap(sent, "row", chip)))
    done = [early(part, scale, saved_hidden.dtype) for part in parts[:EARLY]]
    input_grad = finish(done, parts[EARLY:], scale, saved_hidden.dtype)
    weight_grad = weight_product(
        at,
        [mine[0], mine[2], mate[0], mate[2], mine[1], mine[3], mate[1], mate[3]],
        grads,
        [y_three, y_s2],
    )
    return input_grad, weight_grad


def local(grad_out, saved_hidden, down_weight):
    sizes = [lax.axis_size(a) for a in ("dp", "row", "col")]
    if sizes[0] == 2 and sizes[1] == 2 * CORES and sizes[2] == sizes[1]:
        return paired(grad_out, saved_hidden, down_weight)
    return native(grad_out, saved_hidden, down_weight)


def solution(mesh):
    placed = (P(("dp", "col"), "row"), P(("dp", "row"), "col"), P("col", "row"))
    return jax.shard_map(
        local,
        mesh=mesh,
        in_specs=placed,
        out_specs=(P(("dp", "row"), "col"), P(("col", "dp"), "row")),
        check_vma=False,
    )
```

```python
import functools
import math

import jax
import jax.numpy as jnp
from jax import lax
from jax.experimental import pallas as pl
from jax.experimental.pallas import tpu as pltpu
from jax.sharding import PartitionSpec as P


CORES = 2
LOADS = 3
EARLY = 1
STEPS = (8, 8, 6, 4)
ACROSS = 1
SHARES = (12, 13, 13, 14)
CHUNKS = len(SHARES)
NT = (((1,), (1,)), ((), ()))
TN = (((0,), (0,)), ((), ()))
SMALL = 12 * 2**20
SPLIT = 8
LANES = 128
WIDE_LIMIT = 28 * 2**20
GRAD_MOST = 6.0
WEIGHT_MOST = 0.0625
POWER = 8
TOP = 120.0


def native(grad_out, saved_hidden, down_weight):
    local_rows = saved_hidden.shape[0]
    gathered_all = lax.all_gather(grad_out, ("dp", "col"), axis=0, tiled=True)
    copy_count = lax.axis_size("dp")
    row_count = lax.axis_size("row")
    copy_rows = gathered_all.shape[0] // copy_count
    grad_copy = lax.dynamic_slice_in_dim(
        gathered_all, lax.axis_index("dp") * copy_rows, copy_rows, 0
    )
    hidden_parts = lax.all_to_all(saved_hidden, "dp", split_axis=1, concat_axis=0, tiled=True)
    hidden_stack = lax.all_gather(hidden_parts, "row", axis=0, tiled=True)
    hidden_grid = hidden_stack.reshape(row_count, copy_count, local_rows, hidden_stack.shape[1])
    grad_grid = gathered_all.reshape(copy_count, row_count, local_rows, gathered_all.shape[1])
    weight_grad = jnp.einsum(
        "rdtk,drtn->kn", hidden_grid, grad_grid, preferred_element_type=jnp.float32
    )
    input_grad = lax.psum_scatter(
        lax.dot_general(
            grad_copy, down_weight, (((1,), (1,)), ((), ())), preferred_element_type=jnp.float32
        ),
        "row",
        scatter_dimension=0,
        tiled=True,
    )
    return (input_grad.astype(jnp.bfloat16), weight_grad.astype(jnp.bfloat16))


def encode(value, scale):
    scaled = value * scale
    square = scaled * scaled
    fourth = square * square
    eighth = fourth * fourth
    return jnp.where(scaled < 0, -eighth, eighth).astype(jnp.bfloat16)


def decode(code, scale):
    wide = code.astype(jnp.float32)
    root = jnp.exp(jnp.log(jnp.abs(wide)) * (1.0 / POWER) - math.log(scale))
    return jnp.where(wide < 0, -root, root)


def swap(x, axis, mask):
    n = lax.axis_size(axis)
    return lax.ppermute(x, axis, [(i, i ^ mask) for i in range(n)])


def put_blocks(at, blocks, held):
    rows = blocks[0].shape[0]
    for i, block in enumerate(blocks):
        held[pl.ds(pl.multiple_of(at[i] * rows, rows), rows), :] = block[...]


def start_loads(spans, w, outs, sem):
    copies = []
    for (lo, hi), out in zip(spans, outs):
        step = (hi - lo) // SPLIT
        for i in range(SPLIT):
            part = w.at[pl.ds(lo + i * step, step)]
            copies.append(pltpu.make_async_copy(part, out.at[pl.ds(i * step, step)], sem.at[len(copies)]))
    for c in copies:
        c.start()
    return copies


def load_kernel(spans, at, w, *refs):
    del at
    for c in start_loads(spans, w, refs[:-1], refs[-1]):
        c.wait()


def load(at, weight, spans):
    depth = weight.shape[1]
    return pl.pallas_call(
        functools.partial(load_kernel, spans),
        in_specs=[pl.BlockSpec(memory_space=pltpu.SMEM), pl.BlockSpec(memory_space=pltpu.HBM)],
        out_specs=[pl.BlockSpec(memory_space=pltpu.VMEM)] * len(spans),
        out_shape=[pltpu.VMEM((hi - lo, depth), weight.dtype) for lo, hi in spans],
        scratch_shapes=[pltpu.SemaphoreType.DMA((SPLIT * len(spans),))],
        cost_estimate=pl.CostEstimate(
            flops=0, bytes_accessed=2 * depth * sum(hi - lo for lo, hi in spans), transcendentals=0
        ),
        compiler_params=pltpu.CompilerParams(vmem_limit_bytes=SMALL),
    )(at, pltpu.with_memory_space_constraint(weight, pltpu.HBM))


def product_kernel(n_block, spans, *refs):
    if n_block:
        at, refs = refs[0], refs[1:]
    n = max(n_block, 1)
    blocks, now, refs = refs[:n], refs[n : n + len(spans)], refs[n + len(spans) :]
    keep, give = refs[:2]
    held = blocks[0]
    if n_block:
        held = refs[2]
        put_blocks(at, blocks, held)
    top = keep.shape[0]
    lo = 0
    for ref, (first, last) in zip(now, spans):
        hi = lo + last - first
        part = lax.dot_general(
            held[...], ref[first:last, :], NT, preferred_element_type=jnp.float32
        )
        keep[:, lo:hi] = part[:top]
        give[:, lo:hi] = part[top:]
        lo = hi


def product(grads, now):
    at, blocks = grads if isinstance(grads, tuple) else (None, [])
    rows = 4 * blocks[0].shape[0] if blocks else grads.shape[0]
    depth = now[0][2].shape[1]
    spans = [(first, last) for first, last, _ in now]
    tall = sum(last - first for first, last in spans)
    whole = pl.BlockSpec(memory_space=pltpu.VMEM)
    outs = pl.pallas_call(
        functools.partial(product_kernel, len(blocks), spans),
        in_specs=[pl.BlockSpec(memory_space=pltpu.SMEM)] * (at is not None)
        + [whole] * (max(len(blocks), 1) + len(now)),
        out_specs=[whole] * (2 + (at is not None)),
        out_shape=[jax.ShapeDtypeStruct((rows // 2, tall), jnp.float32)] * 2
        + [pltpu.VMEM((rows, depth), now[0][2].dtype)] * (at is not None),
        cost_estimate=pl.CostEstimate(
            flops=2 * rows * tall * depth, bytes_accessed=2 * tall * depth, transcendentals=0
        ),
        compiler_params=pltpu.CompilerParams(vmem_limit_bytes=SMALL),
    )(
        *([] if at is None else [at]),
        *(blocks or [grads]),
        *[pltpu.with_memory_space_constraint(w, pltpu.VMEM) for _, _, w in now],
    )
    return outs[0], outs[1], outs[-1] if blocks else grads


def finish_kernel(scale, ready, *refs):
    done, refs, (out, staged, sem) = refs[:ready], refs[ready:-3], refs[-3:]
    rows = out.shape[0]
    copies = []
    lo = 0

    def write(tall):
        window = pl.ds(lo, tall)
        copies.append(
            pltpu.make_async_copy(staged.at[:, window], out.at[:, window], sem.at[len(copies)])
        )
        copies[-1].start()

    for chunk in done:
        tall = chunk.shape[1]
        staged[:, lo : lo + tall] = chunk[...]
        write(tall)
        lo += tall
    for keep, got, far in zip(refs[0::3], refs[1::3], refs[2::3]):
        tall = far.shape[1]
        value = (keep[:rows] + got[:rows]) + decode(far[...], scale)
        staged[:, lo : lo + tall] = value.astype(staged.dtype)
        write(tall)
        lo += tall
    for c in copies:
        c.wait()


def finish(done, parts, scale, dtype):
    rows = parts[0][2].shape[0]
    whole = pl.BlockSpec(memory_space=pltpu.VMEM)
    hid = sum(c.shape[1] for c in done) + sum(p[2].shape[1] for p in parts)
    return pl.pallas_call(
        functools.partial(finish_kernel, scale, len(done)),
        in_specs=[whole] * (len(done) + 3 * len(parts)),
        out_specs=pl.BlockSpec(memory_space=pltpu.HBM),
        out_shape=jax.ShapeDtypeStruct((rows, hid), dtype),
        scratch_shapes=[
            pltpu.VMEM((rows, hid), dtype),
            pltpu.SemaphoreType.DMA((len(done) + len(parts),)),
        ],
        cost_estimate=pl.CostEstimate(
            flops=20 * rows * hid, bytes_accessed=14 * rows * hid, transcendentals=0
        ),
        compiler_params=pltpu.CompilerParams(vmem_limit_bytes=SMALL),
    )(*done, *[x for p in parts for x in p])


def early_kernel(scale, keep, got, far, out):
    rows = out.shape[0]
    out[...] = ((keep[:rows] + got[:rows]) + decode(far[...], scale)).astype(out.dtype)


def early(part, scale, dtype):
    rows, tall = part[2].shape
    whole = pl.BlockSpec(memory_space=pltpu.VMEM)
    return pl.pallas_call(
        functools.partial(early_kernel, scale),
        in_specs=[whole] * 3,
        out_specs=whole,
        out_shape=pltpu.VMEM((rows, tall), dtype),
        cost_estimate=pl.CostEstimate(
            flops=20 * rows * tall, bytes_accessed=14 * rows * tall, transcendentals=0
        ),
        compiler_params=pltpu.CompilerParams(vmem_limit_bytes=SMALL),
    )(*part)


def weight_kernel(n_hid, pieces, at, *refs):
    rows = refs[0].shape[0]
    hidden, own, peers = refs[:n_hid], refs[n_hid], refs[n_hid + 1 : -4]
    out, held, slots, sem = refs[-4:]
    half = own.shape[0]
    held[:half, :] = own[...]
    for peer, places in zip(peers, ((0, 2, 1), (3,))):
        for i, place in enumerate(places):
            start = pl.multiple_of(half + at[place] * rows, rows)
            held[pl.ds(start, rows), :] = peer[i * rows : (i + 1) * rows]
    copies = []
    for n, (top, end, lo, hi) in enumerate(pieces):
        if n >= 2:
            copies[n - 2].wait()
        stacked = jnp.concatenate([h[:, top:end] for h in hidden])
        slot = slots.at[n % 2, : end - top, : hi - lo]
        slot[...] = lax.dot_general(
            stacked, held[:, lo:hi], TN, preferred_element_type=jnp.float32
        ).astype(out.dtype)
        place = out.at[pl.ds(top, end - top), pl.ds(lo, hi - lo)]
        copies.append(pltpu.make_async_copy(slot, place, sem.at[n]))
        copies[-1].start()
    for c in copies[-2:]:
        c.wait()


def weight_product(at, hidden, own, peers):
    rows, hid = hidden[0].shape
    depth = own.shape[1]
    tokens = rows * len(hidden)
    tiles = hid // LANES
    edges = [LANES * (tiles * sum(STEPS[:i]) // sum(STEPS)) for i in range(len(STEPS) + 1)]
    pieces = [(top, end, lo, lo + depth // ACROSS) for top, end in zip(edges, edges[1:]) for lo in range(0, depth, depth // ACROSS)]
    tall, wide = max(end - top for top, end, _, _ in pieces), depth // ACROSS
    whole = pl.BlockSpec(memory_space=pltpu.VMEM)
    return pl.pallas_call(
        functools.partial(weight_kernel, len(hidden), pieces),
        in_specs=[pl.BlockSpec(memory_space=pltpu.SMEM)] + [whole] * (len(hidden) + 1 + len(peers)),
        out_specs=pl.BlockSpec(memory_space=pltpu.HBM),
        out_shape=jax.ShapeDtypeStruct((hid, depth), hidden[0].dtype),
        scratch_shapes=[
            pltpu.VMEM((tokens, depth), hidden[0].dtype),
            pltpu.VMEM((2, tall, wide), hidden[0].dtype),
            pltpu.SemaphoreType.DMA((len(pieces),)),
        ],
        cost_estimate=pl.CostEstimate(
            flops=2 * tokens * hid * depth, bytes_accessed=2 * hid * depth, transcendentals=0
        ),
        compiler_params=pltpu.CompilerParams(vmem_limit_bytes=WIDE_LIMIT),
    )(at, *hidden, own, *peers)


def paired(grad_out, saved_hidden, down_weight):
    d, r, z = (lax.axis_index(a) for a in ("dp", "row", "col"))
    chip = CORES
    rows = saved_hidden.shape[0]
    hid, depth = down_weight.shape
    half = hid // 2

    pair = swap(grad_out, "col", 1)
    rev = swap(grad_out, "col", 3)
    s2 = swap(rev, "col", 1)
    three = jnp.concatenate([grad_out, rev, pair])
    y_three = swap(three, "dp", 1)
    y_s2 = swap(s2, "dp", 1)
    h_give = lax.dynamic_slice_in_dim(saved_hidden, (1 - d) * half, half, 1)
    h_mine = lax.dynamic_slice_in_dim(saved_hidden, d * half, half, 1)
    h_peer = swap(h_give, "dp", 1)
    h_far = swap(h_mine, "row", chip)
    h_peer_far = swap(h_peer, "row", chip)
    mine = [h_mine, h_peer, h_far, h_peer_far]
    mate = [swap(h, "row", 1) for h in mine]

    ks = [r ^ z ^ m for m in (0, 1, 3, 2)]
    at = jnp.stack([((k & 1) << 1) | (k >> 1) for k in ks]).astype(jnp.int32)
    scale = 2.0 ** (TOP / POWER) / (CORES * depth * GRAD_MOST * WEIGHT_MOST)
    tiles = hid // LANES
    edges = [LANES * (tiles * sum(SHARES[:i]) // sum(SHARES)) for i in range(CHUNKS + 1)]
    cuts = [LANES * (tiles * i // LOADS) for i in range(LOADS + 1)]
    loaded = []
    for lo, hi in zip(cuts, cuts[1:]):
        (part,) = load(at, down_weight, [(lo, hi)])
        loaded.append((lo, hi, part))
    grads = (at, [grad_out, pair, rev, s2])
    parts = []
    for lo, hi in zip(edges, edges[1:]):
        now = [(max(lo, a) - a, min(hi, b) - a, w) for a, b, w in loaded if a < hi and lo < b]
        keep, give, grads = product(grads, now)
        got = swap(give, "row", 1)
        sent = encode(keep[rows:] + got[rows:], scale)
        parts.append((keep, got, swap(sent, "row", chip)))
    done = [early(part, scale, saved_hidden.dtype) for part in parts[:EARLY]]
    input_grad = finish(done, parts[EARLY:], scale, saved_hidden.dtype)
    weight_grad = weight_product(
        at,
        [mine[0], mine[2], mate[0], mate[2], mine[1], mine[3], mate[1], mate[3]],
        grads,
        [y_three, y_s2],
    )
    return input_grad, weight_grad


def local(grad_out, saved_hidden, down_weight):
    sizes = [lax.axis_size(a) for a in ("dp", "row", "col")]
    if sizes[0] == 2 and sizes[1] == 2 * CORES and sizes[2] == sizes[1]:
        return paired(grad_out, saved_hidden, down_weight)
    return native(grad_out, saved_hidden, down_weight)


def solution(mesh):
    placed = (P(("dp", "col"), "row"), P(("dp", "row"), "col"), P("col", "row"))
    return jax.shard_map(
        local,
        mesh=mesh,
        in_specs=placed,
        out_specs=(P(("dp", "row"), "col"), P(("col", "dp"), "row")),
        check_vma=False,
    )
```
